32 devices in a mesh: seg: 4 (over z), grp: 4 (over y, x), pair: 2 (over core).
Axes of the slice: x: 2, y: 2, z: 4, core: 2. Of those that a mesh axis runs over, the one named last changes fastest.
Arguments:
- observations: float32 [128, 256], P(('grp', 'seg')), may hold values from -6 to 6
- masks: int32 [128, 256], P(('grp', 'seg')), may hold values 0 or 1
- gains: float32 [256], replicated, may hold values from 0.05 to 0.5
- transition: float32 [256, 256], replicated, may hold values from -1 to 1, as said below
- smoother_scale: float32 [256], replicated, may hold values from 0.995 to 0.9999
- initial_mean: float32 [256], replicated, may hold values from -8 to 8
Outputs:
- filtered: float32 [128, 256], P(('grp', 'seg'), 'pair')
- smoothed: float32 [128, 256], P(('grp', 'seg'), 'pair')
The draws below stay inside these ranges and needn't reach their ends.
Inputs may be any that keep to these rules, and one draw needn't show every extreme that they name: Each column of transition is a unit vector scaled by a factor in (0, 1); the columns are orthogonal.
All inputs are finite; a program needn't handle non-finite values. No bound on the sum of `masks` on one device may be relied on, other than what follows from the above.
Results may differ from the reference program's by a relative error of at most 0.0003.
Values sent between devices are 32-bit elements; how exact they have to be, the bound alone decides.
No kernel may reach another device: no remote copies, remote signals or barrier semaphores. Data moves between devices by JAX's collectives and lax.ppermute only.
A program may use at most 64 MiB of HBM per device.

```python
import math
import jax
import jax.numpy as jnp
from jax import lax

M = 256
DAYS = 128


def draw_transition(key, part):
    key_basis, key_share, key_fast = jax.random.split(jax.random.fold_in(key, 11), 3)
    normals = jax.random.normal(key_basis, (M, M), jnp.float32)
    basis, upper = jnp.linalg.qr(normals)
    share = 0.5
    picks = jax.random.uniform(key_share, (M,), jnp.float32)
    slow_rate = jnp.exp(jnp.log(0.2) / DAYS)
    fast_rate = jnp.exp(-1.0 / jax.random.uniform(key_fast, (M,), jnp.float32, 30.0, 50.0))
    rates = jnp.where(picks < share, slow_rate, fast_rate)
    return (basis * rates[None, :]).astype(jnp.float32)


def with_ends(result, own_key, least, high):
    spot = [jax.random.randint(jax.random.fold_in(own_key, axis), (), 0, length) for axis, length in enumerate(result.shape)]
    main_axis = result.shape.index(max(result.shape))
    beside = spot[:main_axis] + [(spot[main_axis] + 1) % result.shape[main_axis]] + spot[main_axis + 1:]
    return result.at[tuple(spot)].set(least).at[tuple(beside)].set(high)


def block_scale(stream_key, shape, cuts, smallest, high):
    def one(dim, blocks):
        steps = jax.random.uniform(jax.random.fold_in(jax.random.fold_in(stream_key, 6), dim), (blocks,), jnp.float32, smallest / len(cuts), high / len(cuts))
        return jnp.repeat(jnp.exp(steps), shape[dim] // blocks).reshape((-1,) + (1,) * (len(shape) - dim - 1))

    factor_of = one(*cuts[0])
    for cut in cuts[1:]:
        factor_of = factor_of * one(*cut)
    return factor_of


def centred(own_key, dims, width, most, cuts=(), kind=jnp.bfloat16):
    array = width * jax.random.normal(own_key, dims, jnp.float32)
    if cuts:
        array = array * block_scale(own_key, dims, cuts, -0.22, 0.18)
    return jnp.clip(array, -most, most).astype(kind)


def setup_inputs(seed: int = 0) -> dict:
    seeds = jax.random.split(jax.random.key(seed), 7)
    observations = centred(seeds[0], (DAYS, M), 1.0, 6.0, ((0, 16),), jnp.float32)
    masks = with_ends((jax.random.randint(seeds[1], (DAYS, M), 0, 32) < 1).astype(jnp.int32), jax.random.fold_in(seeds[1], 1), 0, 1)
    gains = jnp.clip(jnp.exp(jax.random.uniform(seeds[2], (M,), jnp.float32, math.log(0.05), math.log(0.5))), 0.05, 0.5)
    transition = draw_transition(jax.random.fold_in(seeds[6], 71), 0)
    smoother_scale = jnp.clip(jnp.exp(jax.random.uniform(seeds[4], (M,), jnp.float32, math.log(0.995), math.log(0.9999))), 0.995, 0.9999)
    initial_mean = centred(seeds[5], (M,), 2.0, 8.0, (), jnp.float32)
    return dict(observations=observations, masks=masks, gains=gains, transition=transition, smoother_scale=smoother_scale, initial_mean=initial_mean)


def reference(observations, masks, gains, transition, smoother_scale, initial_mean):
    highest = lax.Precision.HIGHEST
    observed = masks.astype(jnp.float32) * gains[None, :]
    retain = 1.0 - observed
    forcing = observed * observations
    smoother_gain = smoother_scale[:, None] * transition.T

    def forward_step(mean_prev, row_pair):
        retain_row, forcing_row = row_pair
        mean_next = retain_row * jnp.dot(transition, mean_prev, precision=highest) + forcing_row
        return (mean_next, mean_next)
    unused, filtered = lax.scan(forward_step, initial_mean, (retain, forcing))
    boundary = jnp.dot(transition, filtered[-1], precision=highest)

    def backward_step(smooth_next, mean_here):
        predicted = jnp.dot(transition, mean_here, precision=highest)
        smooth_here = mean_here + jnp.dot(smoother_gain, smooth_next - predicted, precision=highest)
        return (smooth_here, smooth_here)
    unused_two, smoothed = lax.scan(backward_step, boundary, filtered, reverse=True)
    return (filtered, smoothed)
```

```python
import functools
import jax
import jax.numpy as jnp
from jax import lax
from jax.experimental import pallas as pl
from jax.experimental.pallas import tpu as pltpu
from jax.sharding import PartitionSpec as P

HIGHEST = lax.Precision.HIGHEST
F32 = jnp.float32
BF16 = jnp.bfloat16
ROWS = 8
PARAMS = pltpu.CompilerParams(vmem_limit_bytes=20 * 2**20)


def split(x):
    high = x.astype(BF16)
    return high, (x - high.astype(F32)).astype(BF16)


def dot3(x, high, low):
    x_high, x_low = split(x)
    n = x.shape[0]
    both = jnp.dot(jnp.concatenate([x_high, x_low], 0), high, preferred_element_type=F32)
    return both[:n] + (both[n:] + jnp.dot(x_high, low, preferred_element_type=F32))


def powers_kernel(t_ref, scale_ref, th_ref, tl_ref, high_ref, low_ref, keep_ref):
    count = high_ref.shape[0]
    t = t_ref[...]
    t_t = jnp.transpose(t)
    th_ref[...], tl_ref[...] = split(t_t)
    keep_ref[...] = 1.0 - scale_ref[...] * jnp.sum(t * t, axis=0, keepdims=True)
    power = t * scale_ref[...]
    for k in range(count):
        high_ref[k], low_ref[k] = split(power)
        if k + 1 < count:
            power = jnp.dot(power, power, precision=HIGHEST, preferred_element_type=F32)


def smoother_kernel(
    here_ref, data_ref, gains_ref, mean_ref, th_ref, tl_ref, high_ref, low_ref, keep_ref,
    filt_ref, smooth_ref, s_ref,
):
    blocks = data_ref.shape[0]
    width = data_ref.shape[-1]
    days = blocks * ROWS
    here = here_ref[0]

    @pl.when(here_ref[1] > 0)
    def work():
        row = lax.broadcasted_iota(jnp.int32, (ROWS, width), 0)

        def forward(block, x):
            at = lax.bitwise_xor(block, here)
            observed = data_ref[at, 1] * gains_ref[...]
            retain = 1.0 - observed
            forcing = observed * data_ref[at, 0]
            out = jnp.zeros((ROWS, width), F32)
            for k in range(ROWS):
                x = retain[k : k + 1] * dot3(x, th_ref[...], tl_ref[...]) + forcing[k : k + 1]
                out = jnp.where(row == k, x, out)
            s_ref[pl.ds(pl.multiple_of(block * ROWS, ROWS), ROWS)] = out
            return x

        last = lax.fori_loop(
            0, blocks, forward, jnp.broadcast_to(mean_ref[...], (ROWS, width))
        )
        own = pl.ds(pl.multiple_of(here * ROWS, ROWS), ROWS)
        filt_ref[...] = s_ref[own]
        boundary = dot3(last, th_ref[...], tl_ref[...])
        entering = dot3(boundary, high_ref[0], low_ref[0])
        every = pl.ds(0, days)
        s_ref[every] = s_ref[every] * keep_ref[...]
        tail = pl.ds(days - ROWS, ROWS)
        s_ref[tail] = s_ref[tail] + jnp.where(row == ROWS - 1, entering, 0.0)
        s_ref[pl.ds(days, days)] = jnp.zeros((days, width), F32)
        step, k = 1, 0
        while step < ROWS:
            s_ref[every] = s_ref[every] + dot3(s_ref[pl.ds(step, days)], high_ref[k], low_ref[k])
            step, k = 2 * step, k + 1
        k = high_ref.shape[0] - 1
        step = days // 2
        while step >= ROWS:
            base = pl.multiple_of(here * ROWS, ROWS)
            s_ref[pl.ds(base, step)] = s_ref[pl.ds(base, step)] + dot3(
                s_ref[pl.ds(base + step, step)], high_ref[k], low_ref[k]
            )
            step, k = step // 2, k - 1
        smooth_ref[...] = s_ref[own]

    @pl.when(here_ref[1] == 0)
    def idle():
        filt_ref[...] = jnp.zeros(filt_ref.shape, F32)
        smooth_ref[...] = jnp.zeros(smooth_ref.shape, F32)


def swap(x, axis, flip):
    return lax.ppermute(x, axis, [(i, i ^ flip) for i in range(lax.axis_size(axis))])


def shards(observations, masks, gains, transition, smoother_scale, initial_mean):
    width = transition.shape[0]
    seg_count, grp_count = lax.axis_size("seg"), lax.axis_size("grp")
    blocks = seg_count * grp_count
    days = blocks * ROWS
    vmem = pl.BlockSpec(memory_space=pltpu.VMEM)
    smem = pl.BlockSpec(memory_space=pltpu.SMEM)
    count = days.bit_length() - 1
    scale_row = smoother_scale[None, :]
    th, tl, high, low, keep = pl.pallas_call(
        powers_kernel,
        out_shape=(
            jax.ShapeDtypeStruct((width, width), BF16),
            jax.ShapeDtypeStruct((width, width), BF16),
            jax.ShapeDtypeStruct((count, width, width), BF16),
            jax.ShapeDtypeStruct((count, width, width), BF16),
            jax.ShapeDtypeStruct((1, width), F32),
        ),
        in_specs=[vmem] * 2,
        out_specs=[vmem] * 5,
        compiler_params=PARAMS,
    )(transition, scale_row)
    data = jnp.stack([observations, masks.astype(F32)])[None]
    for axis, size in (("seg", seg_count), ("grp", grp_count)):
        flip = 1
        while flip < size:
            data = jnp.concatenate([data, swap(data, axis, flip)], 0)
            flip *= 2
    pair = lax.axis_index("pair")
    here = lax.axis_index("grp") * seg_count + lax.axis_index("seg")
    filtered, smoothed = pl.pallas_call(
        smoother_kernel,
        out_shape=(jax.ShapeDtypeStruct((ROWS, width), F32),) * 2,
        in_specs=[smem] + [vmem] * 8,
        out_specs=[vmem] * 2,
        scratch_shapes=[pltpu.VMEM((2 * days, width), F32)],
        compiler_params=PARAMS,
    )(jnp.stack([here, pair]).astype(jnp.int32), data, gains[None, :], initial_mean[None, :], th, tl, high, low, keep)
    half = width // lax.axis_size("pair")
    both = jnp.concatenate([filtered, smoothed], 0)
    got = lax.ppermute(both[:, :half], "pair", [(0, 1), (1, 0)])
    mine = jnp.where(pair == 1, both[:, half:], got)
    return mine[:ROWS], mine[ROWS:]


def solution(mesh):
    return jax.shard_map(
        shards,
        mesh=mesh,
        in_specs=(P(("grp", "seg"), None), P(("grp", "seg"), None), P(), P(), P(), P()),
        out_specs=(P(("grp", "seg"), "pair"), P(("grp", "seg"), "pair")),
        check_vma=False,
    )
```

```python
import functools
import jax
import jax.numpy as jnp
from jax import lax
from jax.experimental import pallas as pl
from jax.experimental.pallas import tpu as pltpu
from jax.sharding import PartitionSpec as P

HIGHEST = lax.Precision.HIGHEST
F32 = jnp.float32
BF16 = jnp.bfloat16
ROWS = 8
LANES = 128
BITS = 4
VMEM = pl.BlockSpec(memory_space=pltpu.VMEM)
SMEM = pl.BlockSpec(memory_space=pltpu.SMEM)
ANY = pl.BlockSpec(memory_space=pl.ANY)
HBM = pl.BlockSpec(memory_space=pltpu.HBM)


def params(mib):
    return pltpu.CompilerParams(vmem_limit_bytes=mib * 2**20)


def split(x):
    high = x.astype(BF16)
    return high, (x - high.astype(F32)).astype(BF16)


def dot3(x, high, low):
    x_high, x_low = split(x)
    n = x.shape[0]
    both = jnp.dot(jnp.concatenate([x_high, x_low], 0), high, preferred_element_type=F32)
    return both[:n] + (both[n:] + jnp.dot(x_high, low, preferred_element_type=F32))


def down_sum(x):
    for shift in (4, 2, 1):
        x = x + pltpu.roll(x, shift, 0)
    return x


def load_kernel(
    obs_hbm, mask_hbm, t_hbm, scale_hbm, gains_hbm, mean_hbm, data_ref, t_ref, rows_ref, mask_ref, in_ref, sems
):
    targets = (data_ref.at[0, 0], mask_ref, t_ref, in_ref.at[2], in_ref.at[0], in_ref.at[1])
    sources = (obs_hbm, mask_hbm, t_hbm, scale_hbm, gains_hbm, mean_hbm)
    copies = [
        pltpu.make_async_copy(source, target, sems.at[k])
        for k, (source, target) in enumerate(zip(sources, targets))
    ]
    for copy in copies:
        copy.start()
    for copy in copies:
        copy.wait()
    data_ref[0, 1] = mask_ref[...].astype(F32)
    for k in range(3):
        rows_ref[k : k + 1] = in_ref[k]


def setup_kernel(
    t_ref, in_ref, tt_ref, th_ref, tl_ref, rows_ref, kept_ref, power_ref, high_ref, low_ref
):
    width = t_ref.shape[0]
    t = t_ref[...]
    t_t = jnp.transpose(t)
    tt_ref[...] = t_t
    th_ref[...], tl_ref[...] = split(t_t)
    scale = in_ref[2:3]
    keep = 1.0 - scale * jnp.sum(t * t, axis=0, keepdims=True)
    rows_ref[...] = in_ref[...]
    rows_ref[2:3] = keep
    kept = jnp.transpose(jnp.broadcast_to(1.0 - in_ref[0:1], (ROWS, width)))
    kept_ref[...] = jnp.broadcast_to(kept[:, :1], (width, LANES))
    power = t * scale
    power_ref[...] = power
    high_ref[0], low_ref[0] = split(power)


def power_kernel(gate, in_ref, power_ref, high_ref, low_ref):
    del gate
    power = in_ref[...]
    for k in range(high_ref.shape[0]):
        power = jnp.dot(power, power, precision=HIGHEST, preferred_element_type=F32)
        high_ref[k], low_ref[k] = split(power)
    power_ref[...] = power


def smoother_kernel(steps, here_ref, data_ref, rows_ref, kept_ref, t_ref, tt_ref, th_ref, tl_ref, *refs):
    highs, lows = refs[: len(steps)], refs[len(steps) : 2 * len(steps)]
    send_ref, mine_ref, bits_ref, retain_ref, force_ref, f_ref, s_ref = refs[2 * len(steps) :]
    blocks = data_ref.shape[0]
    width = data_ref.shape[-1]
    days = blocks * ROWS
    here = here_ref[0]
    half = width // 2
    tiles = width // ROWS
    powers = [(high, low, k) for high, low, n in zip(highs, lows, steps) for k in range(n)]

    def advance(x, k):
        high, low, at = powers[k]
        return dot3(x, high[at], low[at])

    @pl.when(here_ref[1] > 0)
    def work():
        row = lax.broadcasted_iota(jnp.int32, (ROWS, width), 0)
        gains = rows_ref[0:1]
        group = min(ROWS, blocks)

        def prepare(word, carry):
            packed = jnp.zeros((ROWS, width), jnp.int32)
            for q in range(group):
                block = word * group + q
                at = lax.bitwise_xor(block, here)
                mask = data_ref[at, 1]
                observed = mask * gains
                retain_ref[block] = 1.0 - observed
                force_ref[block] = observed * data_ref[at, 0]
                even = jnp.where((row & 1) == 0, mask, 0.0).astype(jnp.int32)
                packed = packed | (even << ((row >> 1) + BITS * q))
            for shift in (4, 2):
                packed = packed | pltpu.roll(packed, shift, 0)
            bits_ref[word] = jnp.broadcast_to(jnp.transpose(packed)[:, :1], (width, LANES))
            return carry

        lax.fori_loop(0, blocks // group, prepare, 0)
        force = force_ref[...]
        ahead = dot3(force.reshape(days, width), th_ref[...], tl_ref[...])
        ahead = pltpu.roll(ahead, 1, 0).reshape(blocks, ROWS, width)
        odd = (lax.broadcasted_iota(jnp.int32, (blocks, ROWS, width), 1) & 1) == 1
        force_ref[...] = jnp.where(odd, retain_ref[...] * ahead, 0.0) + force
        f_ref[...] = jnp.zeros(f_ref.shape, F32)
        mean = rows_ref[1:2]
        f_ref[ROWS - 1 : ROWS] = mean

        def forward(block, x):
            word, first = block // group, 31 - BITS * (block % group)
            out = jnp.zeros((ROWS, width), F32)
            for k in range(0, ROWS, 2):
                left, right = x[:, :half], x[:, half:]
                total_left = jnp.zeros((ROWS, half), F32)
                total_right = total_left
                for j in range(tiles):
                    at = slice(ROWS * j, ROWS * (j + 1))
                    product = t_ref[at, :half] * left + t_ref[at, half:] * right
                    u = jnp.broadcast_to(jnp.sum(product, axis=1, keepdims=True), (ROWS, half))
                    seen = bits_ref[word, at] << (first - k // 2)
                    u = jnp.where(seen < 0, u * kept_ref[at], u)
                    total_left = total_left + tt_ref[at, :half] * u
                    total_right = total_right + tt_ref[at, half:] * u
                z = down_sum(jnp.concatenate([total_left, total_right], 1))
                x = retain_ref[block, k + 1 : k + 2] * z + force_ref[block, k + 1 : k + 2]
                out = jnp.where(row == k + 1, x, out)
            f_ref[pl.ds(pl.multiple_of(ROWS * block + ROWS, ROWS), ROWS)] = out
            return x

        lax.fori_loop(0, blocks, forward, jnp.broadcast_to(mean, (ROWS, width)))
        every = pl.ds(ROWS, days)
        ahead = dot3(f_ref[pl.ds(ROWS - 1, days + ROWS)], th_ref[...], tl_ref[...])
        boundary = ahead[days:]
        even_days = retain_ref[...].reshape(days, width) * ahead[:days] + force_ref[...].reshape(days, width)
        day = lax.broadcasted_iota(jnp.int32, (days, width), 0)
        filtered = jnp.where((day & 1) == 0, even_days, f_ref[every])
        f_ref[every] = filtered
        s_ref[pl.ds(0, days)] = filtered * rows_ref[2:3]
        s_ref[pl.ds(days, ROWS)] = jnp.where(row == 0, boundary, 0.0)
        s_ref[pl.ds(days + ROWS, days - ROWS)] = jnp.zeros((days - ROWS, width), F32)
        entering = advance(boundary, 3)
        step, k = 1, 0
        while step < ROWS:
            s_ref[pl.ds(0, days)] = s_ref[pl.ds(0, days)] + advance(s_ref[pl.ds(step, days)], k)
            step, k = 2 * step, k + 1
        tail = pl.ds(days - ROWS, ROWS)
        s_ref[tail] = s_ref[tail] + jnp.where(row == 0, entering, 0.0)
        s_ref[pl.ds(days, ROWS)] = jnp.zeros((ROWS, width), F32)
        base = pl.multiple_of(here * ROWS, ROWS)
        k = len(powers) - 1
        step = days // 2
        while step >= ROWS:
            s_ref[pl.ds(base, step)] = s_ref[pl.ds(base, step)] + advance(s_ref[pl.ds(base + step, step)], k)
            step, k = step // 2, k - 1
        own_filtered = f_ref[pl.ds(base + ROWS, ROWS)]
        own_smoothed = s_ref[pl.ds(base, ROWS)]
        send_ref[:ROWS], mine_ref[:ROWS] = own_filtered[:, :half], own_filtered[:, half:]
        send_ref[ROWS:], mine_ref[ROWS:] = own_smoothed[:, :half], own_smoothed[:, half:]

    @pl.when(here_ref[1] == 0)
    def idle():
        send_ref[...] = jnp.zeros(send_ref.shape, F32)
        mine_ref[...] = jnp.zeros(mine_ref.shape, F32)


def swap(x, axis, flip):
    return lax.ppermute(x, axis, [(i, i ^ flip) for i in range(lax.axis_size(axis))])


def shape(*dims, dtype=F32):
    return jax.ShapeDtypeStruct(dims, dtype)


def hops(mesh_shape):
    return [(axis, 1 << k) for axis in ("seg", "grp") for k in range(mesh_shape[axis].bit_length() - 1)]


def shards(observations, masks, gains, transition, smoother_scale, initial_mean):
    width = transition.shape[0]
    sizes = {axis: lax.axis_size(axis) for axis in ("seg", "grp")}
    blocks = sizes["seg"] * sizes["grp"]
    days = blocks * ROWS
    half = width // 2
    flips = hops(sizes)
    inputs = (
        observations, masks, transition, smoother_scale[None, :], gains[None, :], initial_mean[None, :]
    )
    data, t, rows = pl.pallas_call(
        load_kernel,
        out_shape=(shape(1, 2, ROWS, width), shape(width, width), shape(ROWS, width)),
        in_specs=[HBM] * 6,
        out_specs=[VMEM] * 3,
        scratch_shapes=[
            pltpu.VMEM((ROWS, width), jnp.int32), pltpu.VMEM((3, 1, width), F32), pltpu.SemaphoreType.DMA((6,))
        ],
        compiler_params=params(4),
    )(*(pltpu.with_memory_space_constraint(x, pltpu.HBM) for x in inputs))
    tt, th, tl, rows, kept, power, high, low = pl.pallas_call(
        setup_kernel,
        out_shape=(
            shape(width, width),
            shape(width, width, dtype=BF16), shape(width, width, dtype=BF16),
            shape(ROWS, width), shape(width, LANES), shape(width, width),
            shape(1, width, width, dtype=BF16), shape(1, width, width, dtype=BF16),
        ),
        in_specs=[VMEM] * 2,
        out_specs=[VMEM] * 8,
        compiler_params=params(8),
    )(t, rows)
    highs, lows, steps = [high], [low], [1]
    left = days.bit_length() - 2
    for k, (axis, flip) in enumerate(flips):
        if k > 0:
            count = -(-left // (len(flips) - k))
            left -= count
            power, high, low = pl.pallas_call(
                power_kernel,
                out_shape=(
                    shape(width, width),
                    shape(count, width, width, dtype=BF16),
                    shape(count, width, width, dtype=BF16),
                ),
                in_specs=[ANY, VMEM],
                out_specs=[VMEM] * 3,
                compiler_params=params(8),
            )(data, power)
            highs.append(high)
            lows.append(low)
            steps.append(count)
        other = swap(data, axis, flip)
        data = jnp.concatenate([data, other], 0)
    pair = lax.axis_index("pair")
    here = lax.axis_index("grp") * sizes["seg"] + lax.axis_index("seg")
    send, mine = pl.pallas_call(
        functools.partial(smoother_kernel, steps),
        out_shape=(shape(2 * ROWS, half),) * 2,
        in_specs=[SMEM] + [VMEM] * (7 + 2 * len(steps)),
        out_specs=[VMEM] * 2,
        scratch_shapes=[
            pltpu.VMEM((max(1, blocks // ROWS), width, LANES), jnp.int32),
            pltpu.VMEM((blocks, ROWS, width), F32),
            pltpu.VMEM((blocks, ROWS, width), F32),
            pltpu.VMEM((days + 2 * ROWS, width), F32),
            pltpu.VMEM((2 * days, width), F32),
        ],
        compiler_params=params(12 + blocks // 8),
    )(jnp.stack([here, pair]).astype(jnp.int32), data, rows, kept, t, tt, th, tl, *highs, *lows)
    got = lax.ppermute(send, "pair", [(0, 1), (1, 0)])
    out = jnp.where(pair == 1, mine, got)
    return out[:ROWS], out[ROWS:]


def solution(mesh):
    return jax.shard_map(
        shards,
        mesh=mesh,
        in_specs=(P(("grp", "seg"), None), P(("grp", "seg"), None), P(), P(), P(), P()),
        out_specs=(P(("grp", "seg"), "pair"), P(("grp", "seg"), "pair")),
        check_vma=False,
    )
```

```python
import functools
import jax
import jax.numpy as jnp
from jax import lax
from jax.experimental import pallas as pl
from jax.experimental.pallas import tpu as pltpu
from jax.sharding import PartitionSpec as P

HIGHEST = lax.Precision.HIGHEST
F32 = jnp.float32
BF16 = jnp.bfloat16
ROWS = 8
LANES = 128
BITS = 4
VMEM = pl.BlockSpec(memory_space=pltpu.VMEM)
HBM = pl.BlockSpec(memory_space=pltpu.HBM)


def params(mib):
    return pltpu.CompilerParams(vmem_limit_bytes=mib * 2**20)


def split(x):
    high = x.astype(BF16)
    return high, (x - high.astype(F32)).astype(BF16)


def dot3(x, high, low):
    x_high, x_low = split(x)
    n = x.shape[0]
    both = jnp.dot(jnp.concatenate([x_high, x_low], 0), high, preferred_element_type=F32)
    return both[:n] + (both[n:] + jnp.dot(x_high, low, preferred_element_type=F32))


def down_sum(x):
    for shift in (4, 2, 1):
        x = x + pltpu.roll(x, shift, 0)
    return x


def load_kernel(obs_hbm, mask_hbm, data_ref, mask_ref, sems):
    copies = (
        pltpu.make_async_copy(obs_hbm, data_ref.at[0, 0], sems.at[0]),
        pltpu.make_async_copy(mask_hbm, mask_ref, sems.at[1]),
    )
    for copy in copies:
        copy.start()
    for copy in copies:
        copy.wait()
    data_ref[0, 1] = mask_ref[...].astype(F32)


def setup_kernel(
    t_hbm, scale_hbm, gains_hbm, mean_hbm,
    t_ref, in_ref, power_ref, high_ref, low_ref, sems,
):
    sources = (t_hbm, scale_hbm, gains_hbm, mean_hbm)
    targets = (t_ref, in_ref.at[0], in_ref.at[1], in_ref.at[2])
    copies = [
        pltpu.make_async_copy(source, target, sems.at[k])
        for k, (source, target) in enumerate(zip(sources, targets))
    ]
    for copy in copies:
        copy.start()
    for copy in copies:
        copy.wait()
    power = t_ref[...] * in_ref[0]
    power_ref[...] = power
    high_ref[0], low_ref[0] = split(power)


def layout_kernel(t_ref, in_ref, tt_ref, th_ref, tl_ref, rows_ref, kept_ref):
    width = t_ref.shape[0]
    scale, gains = in_ref[0], in_ref[1]
    t = t_ref[...]
    t_t = jnp.transpose(t)
    tt_ref[...] = t_t
    th_ref[...], tl_ref[...] = split(t_t)
    rows_ref[0:1] = gains
    rows_ref[1:2] = in_ref[2]
    rows_ref[2:3] = 1.0 - scale * jnp.sum(t * t, axis=0, keepdims=True)
    kept = jnp.transpose(jnp.broadcast_to(1.0 - gains, (ROWS, width)))
    kept_ref[...] = jnp.broadcast_to(kept[:, :1], (width, LANES))


def power_kernel(exact, in_ref, power_ref, high_ref, low_ref):
    power = in_ref[...]
    high, low = split(power)
    for k in range(high_ref.shape[0]):
        if exact:
            power = jnp.dot(power, power, precision=HIGHEST, preferred_element_type=F32)
        else:
            power = dot3(power, high, low)
        high, low = split(power)
        high_ref[k], low_ref[k] = high, low
    power_ref[...] = power


def smoother_kernel(steps, data_ref, rows_ref, kept_ref, t_ref, tt_ref, th_ref, tl_ref, *refs):
    highs, lows = refs[: len(steps)], refs[len(steps) : 2 * len(steps)]
    send_ref, mine_ref, bits_ref, retain_ref, force_ref, f_ref, s_ref = refs[2 * len(steps) :]
    blocks = data_ref.shape[0]
    width = data_ref.shape[-1]
    days = blocks * ROWS
    here = lax.axis_index("grp") * lax.axis_size("seg") + lax.axis_index("seg")
    pair = lax.axis_index("pair")
    half = width // 2
    tiles = width // ROWS
    powers = [(high, low, k) for high, low, n in zip(highs, lows, steps) for k in range(n)]

    def advance(x, k):
        high, low, at = powers[k]
        return dot3(x, high[at], low[at])

    @pl.when(pair > 0)
    def work():
        row = lax.broadcasted_iota(jnp.int32, (ROWS, width), 0)
        gains = rows_ref[0:1]
        group = min(ROWS, blocks)

        def prepare(word, carry):
            packed = jnp.zeros((ROWS, width), jnp.int32)
            for q in range(group):
                mask = data_ref[word * group + q, 1]
                even = jnp.where((row & 1) == 0, mask, 0.0).astype(jnp.int32)
                packed = packed | (even << ((row >> 1) + BITS * q))
            for shift in (4, 2):
                packed = packed | pltpu.roll(packed, shift, 0)
            bits_ref[word] = jnp.broadcast_to(jnp.transpose(packed)[:, :1], (width, LANES))
            return carry

        lax.fori_loop(0, blocks // group, prepare, 0)
        f_ref[...] = jnp.zeros(f_ref.shape, F32)
        mean = rows_ref[1:2]
        f_ref[ROWS - 1 : ROWS] = mean

        def factors(block):
            at = lax.bitwise_xor(block, here)
            observed = data_ref[at, 1] * gains
            retain = 1.0 - observed
            force = observed * data_ref[at, 0]
            ahead = pltpu.roll(dot3(force, th_ref[...], tl_ref[...]), 1, 0)
            return retain, jnp.where((row & 1) == 1, retain * ahead, 0.0) + force

        def forward(block, carry):
            x, retain, force = carry
            following = factors(jnp.minimum(block + 1, blocks - 1))
            retain_ref[block], force_ref[block] = retain, force
            at = lax.bitwise_xor(block, here)
            word, first = at // group, 31 - BITS * (at % group)
            out = jnp.zeros((ROWS, width), F32)
            for k in range(0, ROWS, 2):
                left, right = x[:, :half], x[:, half:]
                total_left = jnp.zeros((ROWS, half), F32)
                total_right = total_left
                for j in range(tiles):
                    at = slice(ROWS * j, ROWS * (j + 1))
                    product = t_ref[at, :half] * left + t_ref[at, half:] * right
                    u = jnp.broadcast_to(jnp.sum(product, axis=1, keepdims=True), (ROWS, half))
                    seen = bits_ref[word, at] << (first - k // 2)
                    u = jnp.where(seen < 0, u * kept_ref[at], u)
                    total_left = total_left + tt_ref[at, :half] * u
                    total_right = total_right + tt_ref[at, half:] * u
                z = down_sum(jnp.concatenate([total_left, total_right], 1))
                x = retain[k + 1 : k + 2] * z + force[k + 1 : k + 2]
                out = jnp.where(row == k + 1, x, out)
            f_ref[pl.ds(pl.multiple_of(ROWS * block + ROWS, ROWS), ROWS)] = out
            return (x, *following)

        lax.fori_loop(0, blocks, forward, (jnp.broadcast_to(mean, (ROWS, width)), *factors(0)))
        every = pl.ds(ROWS, days)
        ahead = dot3(f_ref[pl.ds(ROWS - 1, days + ROWS)], th_ref[...], tl_ref[...])
        boundary = ahead[days:]
        even_days = retain_ref[...].reshape(days, width) * ahead[:days] + force_ref[...].reshape(days, width)
        day = lax.broadcasted_iota(jnp.int32, (days, width), 0)
        filtered = jnp.where((day & 1) == 0, even_days, f_ref[every])
        f_ref[every] = filtered
        s_ref[pl.ds(0, days)] = filtered * rows_ref[2:3]
        s_ref[pl.ds(days, ROWS)] = jnp.where(row == 0, boundary, 0.0)
        s_ref[pl.ds(days + ROWS, days - ROWS)] = jnp.zeros((days - ROWS, width), F32)
        entering = advance(boundary, 3)
        step, k = 1, 0
        while step < ROWS:
            s_ref[pl.ds(0, days)] = s_ref[pl.ds(0, days)] + advance(s_ref[pl.ds(step, days)], k)
            step, k = 2 * step, k + 1
        tail = pl.ds(days - ROWS, ROWS)
        s_ref[tail] = s_ref[tail] + jnp.where(row == 0, entering, 0.0)
        s_ref[pl.ds(days, ROWS)] = jnp.zeros((ROWS, width), F32)
        base = pl.multiple_of(here * ROWS, ROWS)
        k = len(powers) - 1
        step = days // 2
        while step >= ROWS:
            s_ref[pl.ds(base, step)] = s_ref[pl.ds(base, step)] + advance(s_ref[pl.ds(base + step, step)], k)
            step, k = step // 2, k - 1
        own_filtered = f_ref[pl.ds(base + ROWS, ROWS)]
        own_smoothed = s_ref[pl.ds(base, ROWS)]
        send_ref[:ROWS], mine_ref[:ROWS] = own_filtered[:, :half], own_filtered[:, half:]
        send_ref[ROWS:], mine_ref[ROWS:] = own_smoothed[:, :half], own_smoothed[:, half:]

    @pl.when(pair == 0)
    def idle():
        send_ref[...] = jnp.zeros(send_ref.shape, F32)
        mine_ref[...] = jnp.zeros(mine_ref.shape, F32)


def swap(x, axis, flip):
    return lax.ppermute(x, axis, [(i, i ^ flip) for i in range(lax.axis_size(axis))])


def shape(*dims, dtype=F32):
    return jax.ShapeDtypeStruct(dims, dtype)


def hops(mesh_shape):
    return [(axis, 1 << k) for axis in ("seg", "grp") for k in range(mesh_shape[axis].bit_length() - 1)]


def squarings(count):
    rest = max(0, count - 2)
    chain = []
    for k in range(1, count - 1):
        take = min(2, rest)
        rest -= take
        if take:
            chain.append((k, take))
    return chain + [(count - 1, 4 + rest)]


def keep_in_hbm(x):
    return pltpu.with_memory_space_constraint(x, pltpu.HBM)


def shards(observations, masks, gains, transition, smoother_scale, initial_mean):
    width = transition.shape[0]
    sizes = {axis: lax.axis_size(axis) for axis in ("seg", "grp")}
    blocks = sizes["seg"] * sizes["grp"]
    days = blocks * ROWS
    half = width // 2
    flips = hops(sizes)
    data = pl.pallas_call(
        load_kernel,
        out_shape=shape(1, 2, ROWS, width),
        in_specs=[HBM] * 2,
        out_specs=VMEM,
        scratch_shapes=[pltpu.VMEM((ROWS, width), jnp.int32), pltpu.SemaphoreType.DMA((2,))],
        compiler_params=params(4),
    )(keep_in_hbm(observations), keep_in_hbm(masks))
    t, vectors, power, high, low = pl.pallas_call(
        setup_kernel,
        out_shape=(
            shape(width, width), shape(3, 1, width), shape(width, width),
            shape(1, width, width, dtype=BF16), shape(1, width, width, dtype=BF16),
        ),
        in_specs=[HBM] * 4,
        out_specs=[VMEM] * 5,
        scratch_shapes=[pltpu.SemaphoreType.DMA((4,))],
        compiler_params=params(8),
    )(*(keep_in_hbm(x) for x in (transition, smoother_scale[None, :], gains[None, :], initial_mean[None, :])))
    tt, th, tl, rows, kept = pl.pallas_call(
        layout_kernel,
        out_shape=(
            shape(width, width), shape(width, width, dtype=BF16), shape(width, width, dtype=BF16),
            shape(ROWS, width), shape(width, LANES),
        ),
        in_specs=[VMEM] * 2,
        out_specs=[VMEM] * 5,
        compiler_params=params(8),
    )(t, vectors)
    highs, lows, steps = [high], [low], [1]
    for k, count in squarings(len(flips)):
        power, high, low = pl.pallas_call(
            functools.partial(power_kernel, k + 1 < len(flips)),
            out_shape=(
                shape(width, width),
                shape(count, width, width, dtype=BF16),
                shape(count, width, width, dtype=BF16),
            ),
            in_specs=[VMEM],
            out_specs=[VMEM] * 3,
            compiler_params=params(8),
        )(power)
        highs.append(high)
        lows.append(low)
        steps.append(count)
    for axis, flip in flips[:-2]:
        other = swap(data, axis, flip)
        data = jnp.concatenate([data, other], 0)
    first, last = len(flips) - 2, len(flips) - 1
    near = swap(data, *flips[first])
    side = swap(data, *flips[last])
    corner = swap(near, *flips[last])
    data = jnp.concatenate([data, near, side, corner], 0)
    pair = lax.axis_index("pair")
    send, mine = pl.pallas_call(
        functools.partial(smoother_kernel, steps),
        out_shape=(shape(2 * ROWS, half),) * 2,
        in_specs=[VMEM] * (7 + 2 * len(steps)),
        out_specs=[VMEM] * 2,
        scratch_shapes=[
            pltpu.VMEM((max(1, blocks // ROWS), width, LANES), jnp.int32),
            pltpu.VMEM((blocks, ROWS, width), F32),
            pltpu.VMEM((blocks, ROWS, width), F32),
            pltpu.VMEM((days + 2 * ROWS, width), F32),
            pltpu.VMEM((2 * days, width), F32),
        ],
        compiler_params=params(12 + blocks // 8),
    )(data, rows, kept, t, tt, th, tl, *highs, *lows)
    got = lax.ppermute(send, "pair", [(0, 1), (1, 0)])
    out = jnp.where(pair == 1, mine, got)
    return out[:ROWS], out[ROWS:]


def solution(mesh):
    return jax.shard_map(
        shards,
        mesh=mesh,
        in_specs=(P(("grp", "seg"), None), P(("grp", "seg"), None), P(), P(), P(), P()),
        out_specs=(P(("grp", "seg"), "pair"), P(("grp", "seg"), "pair")),
        check_vma=False,
    )
```
